256 devices in a mesh: wide: 32 (over x, y, core), narrow: 8 (over z).
Axes of the slice: x: 4, y: 4, z: 8, core: 2. Of those that a mesh axis runs over, the one named last changes fastest.
Arguments:
- panels: float32 [256, 512, 512], P('wide', 'narrow'), may hold values from -0.6 to 0.6
- factors: float32 [64, 512, 512], P('wide', 'narrow'), may hold values from -2 to 2
- member: int32 [64, 4], replicated, may hold values from 0 to 255, as said below
- target: int32 [64, 10], replicated, may hold values from 0 to 31
- ancestors: float32 [32, 512, 512], P('wide', 'narrow'), may hold values from -6 to 6
Outputs:
- updated: float32 [32, 512, 512], P('wide', 'narrow')
The draws below stay inside these ranges and needn't reach their ends.
Inputs may be any that keep to these rules, and one draw needn't show every extreme that they name: `member`: the blocks of supernode s are 4 distinct indices in [(s // 2) * 8, (s // 2 + 1) * 8); every block belongs to exactly one supernode.
All inputs are finite; a program needn't handle non-finite values.
Results may differ from the reference program's by a relative error of at most 0.0003.
Values sent between devices are 32-bit elements; how exact they have to be, the bound alone decides.
No kernel may reach another device: no remote copies, remote signals or barrier semaphores. Data moves between devices by JAX's collectives and lax.ppermute only.
A program may use at most 128 MiB of HBM per device.

```python
import math
import jax
import jax.numpy as jnp
import numpy as np
from jax import lax

W = 512
NB = 4
SUP_DEV = 2
NP = 10
SUPER = 64
BLOCKS = 256
ANC = 32


def draw_factors(key, part):
    diag_key = jax.random.fold_in(key, 11)
    off_key = jax.random.fold_in(key, 12)
    diagonal = jax.random.uniform(diag_key, (SUPER, W), jnp.float32, 0.5, 2.0)
    offdiag = jnp.clip(jax.random.normal(off_key, (SUPER, W, W), jnp.float32), -6.0, 6.0) * (0.5 / jnp.sqrt(jnp.float32(W)))
    eye = jnp.eye(W, dtype=jnp.float32)
    return offdiag * (1.0 - eye)[None] + diagonal[:, :, None] * eye[None]


def draw_member(key, part):
    owners = SUPER // SUP_DEV
    keys = jax.random.split(jax.random.fold_in(key, 21), owners)
    shuffled = jax.vmap(lambda single: jax.random.permutation(single, SUP_DEV * NB))(keys)
    offsets = jnp.arange(owners, dtype=jnp.int32)[:, None] * (SUP_DEV * NB)
    return (shuffled.astype(jnp.int32) + offsets).reshape(SUPER, NB)


def with_ends(drawn, key, smallest, high):
    spot = [jax.random.randint(jax.random.fold_in(key, axis), (), 0, length) for axis, length in enumerate(drawn.shape)]
    longest = drawn.shape.index(max(drawn.shape))
    next_to = spot[:longest] + [(spot[longest] + 1) % drawn.shape[longest]] + spot[longest + 1:]
    return drawn.at[tuple(spot)].set(smallest).at[tuple(next_to)].set(high)


def steps_of(key, extent, cuts, low, top_value):
    level, own = 1.0, jax.random.fold_in(key, 6)
    for dim, parts in cuts:
        draws = jnp.exp(jax.random.uniform(jax.random.fold_in(own, dim), (parts,), jnp.float32, low / len(cuts), top_value / len(cuts)))
        level = level * jnp.repeat(draws, extent[dim] // parts).reshape([-1 if axis == dim else 1 for axis in range(len(extent))])
    return level


def rank_table(number_of, slope):
    loads = [(1 << 20) // math.isqrt(rank ** slope) + 1 for rank in range(1, number_of + 1)]
    spread = 1 + sum(loads) // (1 << 30)
    return np.cumsum(np.array([max(1, weight // spread) for weight in loads]))


def ranked_ids(stream_key, extent, number_of, skew):
    grid = rank_table(number_of, skew)
    lot = jax.random.randint(jax.random.fold_in(stream_key, 1), extent, 0, int(grid[number_of - 1]))
    standing = jnp.searchsorted(jnp.asarray(grid, jnp.int32), lot, side="right")
    return jax.random.permutation(jax.random.fold_in(stream_key, 2), number_of)[standing].astype(jnp.int32)


def gaussian(key, shape, width, most, cuts=(), kind=jnp.bfloat16):
    level = steps_of(key, shape, cuts, -0.22, 0.18) if cuts else 1.0
    values = jax.random.normal(key, shape, jnp.float32) * width * level
    return jnp.minimum(jnp.maximum(values, -most), most).astype(kind)


def setup_inputs(seed: int = 0) -> dict:
    splits = jax.random.split(jax.random.key(seed), 6)
    panels = gaussian(splits[0], (BLOCKS, W, W), 0.1, 0.6, ((0, 32), (1, 8)), jnp.float32)
    factors = draw_factors(jax.random.fold_in(splits[5], 71), 0)
    member = draw_member(jax.random.fold_in(splits[5], 71), 0)
    target = with_ends(ranked_ids(splits[3], (SUPER, NP), ANC, 2), jax.random.fold_in(splits[3], 3), 0, ANC - 1).astype(jnp.int32)
    ancestors = gaussian(splits[4], (ANC, W, W), 1.0, 6.0, ((0, 32), (1, 8)), jnp.float32)
    return {"panels": panels, "factors": factors, "member": member, "target": target, "ancestors": ancestors}


def pair_lists(count):
    left_pick = []
    right_pick = []
    for upper in range(count):
        for lower in range(upper + 1):
            left_pick.append(upper)
            right_pick.append(lower)
    return np.array(left_pick, dtype=np.int32), np.array(right_pick, dtype=np.int32)


def reference(panels, factors, member, target, ancestors):
    left_pick, right_pick = pair_lists(member.shape[1])
    highest = lax.Precision.HIGHEST

    def advance(running, inputs):
        members, factor, targets = inputs
        blocks = panels[members]
        scaled = jnp.einsum("kij,jm->kim", blocks, factor, precision=highest)
        updates = jnp.einsum("pim,pjm->pij", scaled[left_pick], scaled[right_pick], precision=highest)
        onehot = (targets[:, None] == jnp.arange(ANC, dtype=jnp.int32)[None, :]).astype(jnp.float32)
        return running + jnp.einsum("pa,pij->aij", onehot, updates, precision=highest), None

    running, ignored = lax.scan(advance, jnp.zeros((ANC, W, W), jnp.float32), (member, factors, target))
    return ancestors - running
```

```python
import jax
import jax.numpy as jnp
from jax import lax
from jax.experimental import pallas as pl
from jax.experimental.pallas import tpu as pltpu
from jax.sharding import PartitionSpec as P


PAIRS = tuple((k, l) for k in range(4) for l in range(k + 1))
CHUNKS = 4
ANY = pl.BlockSpec(memory_space=pl.ANY)
SMEM = pl.BlockSpec(memory_space=pltpu.SMEM)
VMEM = pl.BlockSpec(memory_space=pltpu.VMEM)
BF, F32 = jnp.bfloat16, jnp.float32


def split(x):
    high = x.astype(BF)
    return high, (x - high.astype(F32)).astype(BF)


def dot3(ah, al, bh, bl, right):
    dims = (((1,), (right,)), ((), ()))

    def dot(a, b):
        return lax.dot_general(a, b, dims, preferred_element_type=F32)

    return dot(ah, bh) + (dot(ah, bl) + dot(al, bh))


def low_lanes(shape):
    return lax.broadcasted_iota(jnp.int32, shape, 1) < 64


def place(meta, s, p):
    tile = meta[10 + s * 10 + p]
    return (tile + meta[1]) & 1, tile >> 1


def scale(x_ref, fh, fl, s):
    xh, xl = split(x_ref[pl.ds(4 * s, 4)].reshape(256, 512))
    return split(dot3(xh, xl, fh[s], fl[s], 0))


def stack(ref, s, side, value):
    for l in range(4):
        ref[s, pl.ds(l * 128 + side * 64, 64)] = value[l * 64 : l * 64 + 64]


def near_kernel(meta, *refs):
    panels, up, down = refs[0], refs[1 : 1 + CHUNKS], refs[1 + CHUNKS : 1 + 2 * CHUNKS]
    fac = refs[1 + 2 * CHUNKS : 9 + 2 * CHUNKS]
    fu4 = refs[9 + 2 * CHUNKS]
    keep, send, diag, fh_out, fl_out, rh_out, rl_out = refs[10 + 2 * CHUNKS : 17 + 2 * CHUNKS]
    x, f, fh, fl, lh, ll, rh, rl, zh, zl, prod, acc, accz, fsem, xsem, osem = refs[17 + 2 * CHUNKS :]
    z = meta[0]
    fcopies = []
    for i, (ref, d) in enumerate(zip(fac[:7], (0, -1, 1, -2, 2, -3, 3))):
        rows = pl.ds(pl.multiple_of(((z + d) & 7) * 64, 64), 64)
        fcopies.append(pltpu.make_async_copy(ref, f.at[:, rows], fsem.at[i]))
    rows4 = pl.ds(pl.multiple_of(((z + 4) & 7) * 64, 64), 64)
    fcopies.append(pltpu.make_async_copy(fu4, f.at[pl.ds(0, 1), rows4], fsem.at[7]))
    fcopies.append(pltpu.make_async_copy(fac[7], f.at[pl.ds(1, 1), rows4], fsem.at[8]))
    for c in fcopies:
        c.start()
    xcopies = []
    per = 8 // CHUNKS
    for piece in range(3):
        for b in range(8):
            src = panels.at[b] if piece == 0 else (up, down)[piece - 1][b // per].at[b % per]
            c = pltpu.make_async_copy(src, x.at[piece, meta[2 + b]], xsem.at[piece * 8 + b])
            c.start()
            xcopies.append(c)
    acc[...] = jnp.zeros_like(acc)
    accz[...] = jnp.zeros_like(accz)
    for c in fcopies:
        c.wait()
    for s in range(2):
        fh[s], fl[s] = split(f[s])
    outs = [pltpu.make_async_copy(a, b, osem.at[i]) for i, (a, b) in enumerate(((fh, fh_out), (fl, fl_out)))]
    for piece in range(3):
        for b in range(8):
            xcopies[piece * 8 + b].wait()
        for s in range(2):
            sh, sl = scale(x.at[piece], fh, fl, s)
            if piece == 0:
                lh[s], ll[s] = sh, sl
                for side in range(2):
                    stack(zh, s, side, sh)
                    stack(zl, s, side, sl)
            else:
                stack(rh, s, piece - 1, sh)
                stack(rl, s, piece - 1, sl)
    outs += [pltpu.make_async_copy(a, b, osem.at[2 + i]) for i, (a, b) in enumerate(((rh, rh_out), (rl, rl_out)))]
    for c in outs:
        c.start()
    low = low_lanes((64, 128))
    for s in range(2):
        prod[pl.ds(0, 256)] = dot3(lh[s], ll[s], rh[s], rl[s], 1)
        for p, (k, l) in enumerate(PAIRS):
            side, chip = place(meta, s, p)
            acc[side, chip, 0] += prod[pl.ds(k * 64, 64), pl.ds(l * 128, 128)]
        prod[...] = dot3(rh[s], rl[s], rh[s], rl[s], 1)
        for p, (k, l) in enumerate(PAIRS):
            side, chip = place(meta, s, p)
            cols = pl.ds(l * 128, 128)
            acc[side, chip, 1] += jnp.where(low, prod[pl.ds(k * 128 + 64, 64), cols], prod[pl.ds(k * 128, 64), cols])
    early = [pltpu.make_async_copy(acc.at[1], send, osem.at[4]), pltpu.make_async_copy(acc.at[0], keep, osem.at[5])]
    for c in early:
        c.start()
    for s in range(2):
        prod[pl.ds(0, 256)] = dot3(lh[s], ll[s], zh[s], zl[s], 1)
        for p, (k, l) in enumerate(PAIRS):
            side, chip = place(meta, s, p)
            accz[side, chip] += jnp.where(low, prod[pl.ds(k * 64, 64), pl.ds(l * 128, 128)], 0.0)
    last = pltpu.make_async_copy(accz, diag, osem.at[6])
    last.start()
    for c in outs + early + [last]:
        c.wait()


def far_kernel(meta, *refs):
    up, down = refs[:CHUNKS], refs[CHUNKS : 2 * CHUNKS]
    fh_in, fl_in, rh_in, rl_in, diag = refs[2 * CHUNKS : 5 + 2 * CHUNKS]
    keep, send = refs[5 + 2 * CHUNKS : 7 + 2 * CHUNKS]
    x, fh, fl, rh, rl, lh, ll, qh, ql, prod, acc, isem, xsem, osem = refs[7 + 2 * CHUNKS :]
    copies = []
    ins = ((fh_in, fh), (fl_in, fl), (rh_in, rh), (rl_in, rl), (diag.at[0], acc.at[0, :, 0]), (diag.at[1], acc.at[1, :, 0]))
    xcopies = []
    per = 8 // CHUNKS
    for piece in range(2):
        for b in range(8):
            src = (up, down)[piece][b // per].at[b % per]
            c = pltpu.make_async_copy(src, x.at[piece, meta[2 + b]], xsem.at[piece * 8 + b])
            c.start()
            xcopies.append(c)
    for i, (a, b) in enumerate(ins):
        c = pltpu.make_async_copy(a, b, isem.at[i])
        c.start()
        copies.append(c)
    acc[:, :, 1] = jnp.zeros((2, 16, 64, 128), F32)
    copies[0].wait()
    copies[1].wait()
    for piece in range(2):
        for b in range(8):
            xcopies[piece * 8 + b].wait()
        for s in range(2):
            sh, sl = scale(x.at[piece], fh, fl, s)
            if piece == 0:
                lh[s], ll[s] = sh, sl
            stack(qh, s, piece, sh)
            stack(ql, s, piece, sl)
    for c in copies[2:]:
        c.wait()
    low = low_lanes((64, 128))
    for s in range(2):
        prod[pl.ds(0, 256)] = dot3(lh[s], ll[s], qh[s], ql[s], 1)
        for p, (k, l) in enumerate(PAIRS):
            side, chip = place(meta, s, p)
            acc[side, chip, 0] += jnp.where(low, 0.0, prod[pl.ds(k * 64, 64), pl.ds(l * 128, 128)])
        prod[...] = dot3(rh[s], rl[s], qh[s], ql[s], 1)
        for p, (k, l) in enumerate(PAIRS):
            side, chip = place(meta, s, p)
            cols = pl.ds(l * 128, 128)
            acc[side, chip, 1] += jnp.where(low, prod[pl.ds(k * 128 + 64, 64), cols], prod[pl.ds(k * 128, 64), cols])
    out = [pltpu.make_async_copy(acc.at[1], send, osem.at[0]), pltpu.make_async_copy(acc.at[0], keep, osem.at[1])]
    for c in out:
        c.start()
    for c in out:
        c.wait()


def final_kernel(meta, anc, e1, eu, ed, own, du, dd, cd, out, acc):
    z = meta[0]
    acc[...] = jnp.zeros_like(acc)
    lane = lax.broadcasted_iota(jnp.int32, (64, 128), 1) // 64
    for src, half, d in ((e1, 0, -1), (e1, 1, 1), (eu, 0, -2), (ed, 1, 2), (own, 0, 0), (du, 0, -3), (dd, 1, 3), (cd, 1, 4)):
        m = (z + d) & 7
        v = src[...]
        v = jnp.where((m & 1) == half, v, pltpu.roll(v, 64, 1))
        acc[m >> 1] += jnp.where(lane == (m & 1), v, 0.0)
    for q in range(4):
        cols = pl.ds(q * 128, 128)
        out[0, :, cols] = anc[0, :, cols] - acc[q]


def shards(panels, factors, member, target, ancestors):
    wide = lax.axis_index("wide")
    z = lax.axis_index("narrow")
    members = lax.dynamic_slice_in_dim(member, wide * 2, 2, 0).reshape(8) - wide * 8
    targets = lax.dynamic_slice_in_dim(target, wide * 2, 2, 0).reshape(20)
    slots = jnp.arange(8, dtype=jnp.int32)
    inverse = jnp.sum(jnp.where(members[:, None] == slots[None, :], slots[:, None], 0), axis=0)
    meta = jnp.concatenate([z[None], (wide & 1)[None], inverse, targets]).astype(jnp.int32)

    def along(x, d):
        return lax.ppermute(x, "narrow", [(i, (i + d) % 8) for i in range(8)])

    def swap(x):
        return lax.ppermute(x, "wide", [(i, i ^ 1) for i in range(32)])

    def scatter(x):
        groups = [[2 * i + c for i in range(16)] for c in range(2)]
        return lax.all_to_all(x, "wide", 0, 0, axis_index_groups=groups, tiled=True)

    per = 8 // CHUNKS
    chunks = [panels[per * c : per * c + per] for c in range(CHUNKS)]
    fu, fd = [factors], [factors]
    for t in range(3):
        fu.append(along(fu[-1], 1))
        fd.append(along(fd[-1], -1))
    fu4 = along(fu[3][:1], 1)
    fd4 = along(fd[3][1:], -1)
    u1 = [along(c, 1) for c in chunks]
    d1 = [along(c, -1) for c in chunks]
    u2 = [along(c, 1) for c in u1]
    d2 = [along(c, -1) for c in d1]

    half = jax.ShapeDtypeStruct((16, 2, 64, 128), F32)
    bf = jax.ShapeDtypeStruct((2, 512, 512), BF)
    dma = pltpu.SemaphoreType.DMA
    keep1, send1, diag, fh, fl, rh, rl = pl.pallas_call(
        near_kernel,
        name="near",
        out_shape=(half, half, jax.ShapeDtypeStruct((2, 16, 64, 128), F32), bf, bf, bf, bf),
        in_specs=[SMEM] + [ANY] * (10 + 2 * CHUNKS),
        out_specs=(ANY,) * 7,
        scratch_shapes=[
            pltpu.VMEM((3, 8, 64, 512), F32),
            pltpu.VMEM((2, 512, 512), F32),
            pltpu.VMEM((2, 512, 512), BF),
            pltpu.VMEM((2, 512, 512), BF),
            pltpu.VMEM((2, 256, 512), BF),
            pltpu.VMEM((2, 256, 512), BF),
            pltpu.VMEM((2, 512, 512), BF),
            pltpu.VMEM((2, 512, 512), BF),
            pltpu.VMEM((2, 512, 512), BF),
            pltpu.VMEM((2, 512, 512), BF),
            pltpu.VMEM((512, 512), F32),
            pltpu.VMEM((2, 16, 2, 64, 128), F32),
            pltpu.VMEM((2, 16, 64, 128), F32),
            dma((9,)),
            dma((24,)),
            dma((7,)),
        ],
    )(meta, panels, *u1, *d1, factors, fu[1], fd[1], fu[2], fd[2], fu[3], fd[3], fd4, fu4)
    r1 = jnp.sum(scatter(keep1 + swap(send1)), axis=0)
    eu, ed = along(r1[1], 1), along(r1[1], -1)

    keep2, send2 = pl.pallas_call(
        far_kernel,
        name="far",
        out_shape=(half, half),
        in_specs=[SMEM] + [ANY] * (5 + 2 * CHUNKS),
        out_specs=(ANY,) * 2,
        scratch_shapes=[
            pltpu.VMEM((2, 8, 64, 512), F32),
            pltpu.VMEM((2, 512, 512), BF),
            pltpu.VMEM((2, 512, 512), BF),
            pltpu.VMEM((2, 512, 512), BF),
            pltpu.VMEM((2, 512, 512), BF),
            pltpu.VMEM((2, 256, 512), BF),
            pltpu.VMEM((2, 256, 512), BF),
            pltpu.VMEM((2, 512, 512), BF),
            pltpu.VMEM((2, 512, 512), BF),
            pltpu.VMEM((512, 512), F32),
            pltpu.VMEM((2, 16, 2, 64, 128), F32),
            dma((6,)),
            dma((16,)),
            dma((2,)),
        ],
    )(meta, *u2, *d2, fh, fl, rh, rl, diag)
    r2 = jnp.sum(scatter(keep2 + swap(send2)), axis=0)
    own, side = r2[0], r2[1]
    du, dd, cd = along(side, 1), along(side, -1), along(own, -2)
    return pl.pallas_call(
        final_kernel,
        name="final",
        out_shape=jax.ShapeDtypeStruct((1, 64, 512), F32),
        in_specs=[SMEM] + [VMEM] * 8,
        out_specs=VMEM,
        scratch_shapes=[pltpu.VMEM((4, 64, 128), F32)],
    )(meta, ancestors, r1[0], eu, ed, own, du, dd, cd)


def solution(mesh):
    return jax.shard_map(
        shards,
        mesh=mesh,
        in_specs=(
            P("wide", "narrow", None),
            P("wide", "narrow", None),
            P(),
            P(),
            P("wide", "narrow", None),
        ),
        out_specs=P("wide", "narrow", None),
        check_vma=False,
    )
```

```python
import jax
import jax.numpy as jnp
from jax import lax
from jax.experimental import pallas as pl
from jax.experimental.pallas import tpu as pltpu
from jax.sharding import PartitionSpec as P


PAIRS = tuple((k, l) for k in range(4) for l in range(k + 1))
BOUNDS = (0, 4, 8)
CHUNKS = len(BOUNDS) - 1
SPOTS = tuple((c, b - BOUNDS[c]) for c in range(CHUNKS) for b in range(BOUNDS[c], BOUNDS[c + 1]))
ANY = pl.BlockSpec(memory_space=pltpu.HBM)
SMEM = pl.BlockSpec(memory_space=pltpu.SMEM)
VMEM = pl.BlockSpec(memory_space=pltpu.VMEM)
BF, F32 = jnp.bfloat16, jnp.float32


def split(x):
    high = x.astype(BF)
    return high, (x - high.astype(F32)).astype(BF)


def low_lanes(shape):
    return lax.broadcasted_iota(jnp.int32, shape, 1) < 64


def prepare(pos, member, target, meta):
    wide = pos[1]
    meta[0] = pos[0]
    meta[1] = wide & 1
    for s in range(2):
        for k in range(4):
            meta[2 + member[k, 2 * wide + s] - 8 * wide] = 4 * s + k
        for p in range(10):
            meta[10 + 10 * s + p] = target[p, 2 * wide + s]


def place(meta, s, p):
    tile = meta[10 + s * 10 + p]
    return (tile + meta[1]) & 1, tile >> 1


def scale(x_ref, f3, s):
    xh, xl = split(x_ref[pl.ds(4 * s, 4)].reshape(256, 512))
    x3 = jnp.concatenate([xh, xh, xl], axis=1)
    return split(lax.dot_general(x3, f3[s], (((1,), (0,)), ((), ())), preferred_element_type=F32))


def put(ref, index, parts):
    for i, part in enumerate(parts):
        ref[(*index, slice(None), pl.ds(512 * i, 512))] = part


def pairwise(left, right):
    return lax.dot_general(left, right, (((1,), (1,)), ((), ())), preferred_element_type=F32)


def tile_of(prod, k, l, upper):
    v = prod[pl.ds(k * 64, 64), pl.ds((l // 2) * 128, 128)]
    return v if (l % 2 == 1) == upper else pltpu.roll(v, 64, 1)


def folded(prod, k, l, lane):
    low, high = tile_of(prod, k, l, False), tile_of(prod, k, l, True)
    return jnp.where(lane, low[:32], high[32:])


def near_kernel(pos, member, target, *refs):
    *refs, meta = refs
    prepare(pos, member, target, meta)
    panels, up, down = refs[0], refs[1 : 1 + CHUNKS], refs[1 + CHUNKS : 1 + 2 * CHUNKS]
    fac = refs[1 + 2 * CHUNKS : 9 + 2 * CHUNKS]
    fu4 = refs[9 + 2 * CHUNKS]
    keep, send, f_out, n_out = refs[10 + 2 * CHUNKS : 14 + 2 * CHUNKS]
    x, f, f3, left, right, prod, acc, fsem, xsem, osem = refs[14 + 2 * CHUNKS :]
    z = meta[0]
    fcopies = []
    for i, (ref, d) in enumerate(zip(fac[:7], (0, -1, 1, -2, 2, -3, 3))):
        rows = pl.ds(pl.multiple_of(((z + d) & 7) * 64, 64), 64)
        fcopies.append(pltpu.make_async_copy(ref, f.at[:, rows], fsem.at[i]))
    rows4 = pl.ds(pl.multiple_of(((z + 4) & 7) * 64, 64), 64)
    fcopies.append(pltpu.make_async_copy(fu4, f.at[pl.ds(0, 1), rows4], fsem.at[7]))
    fcopies.append(pltpu.make_async_copy(fac[7], f.at[pl.ds(1, 1), rows4], fsem.at[8]))
    for c in fcopies:
        c.start()
    xcopies = []
    for piece in range(3):
        for b in range(8):
            src = panels.at[b] if piece == 0 else (up, down)[piece - 1][SPOTS[b][0]].at[SPOTS[b][1]]
            c = pltpu.make_async_copy(src, x.at[piece, meta[2 + b]], xsem.at[piece * 8 + b])
            c.start()
            xcopies.append(c)
    acc[...] = jnp.zeros_like(acc)
    for c in fcopies:
        c.wait()
    for s in range(2):
        high, low = split(f[s])
        for i, part in enumerate((high, low, high)):
            f3[s, pl.ds(512 * i, 512)] = part
    outs = [pltpu.make_async_copy(f3.at[:, pl.ds(0, 1024)], f_out, osem.at[0])]
    outs[0].start()
    for piece in range(3):
        for b in range(8):
            xcopies[piece * 8 + b].wait()
        for s in range(2):
            high, low = scale(x.at[piece], f3, s)
            put(left, (piece, s), (high, high, low))
            put(right, (piece, s), (high, low, high))
    outs.append(pltpu.make_async_copy(left.at[pl.ds(1, 2), :, :, pl.ds(512, 1024)], n_out, osem.at[1]))
    outs[1].start()
    lane = low_lanes((64, 128))
    for s in range(2):
        prod[0] = pairwise(left[0, s], right[1, s])
        prod[1] = pairwise(left[0, s], right[2, s])
        prod[2] = pairwise(left[2, s], right[1, s])
        prod[3] = pairwise(left[1, s], right[2, s])
        prod[4] = pairwise(left[0, s], right[0, s])
        for p, (k, l) in enumerate(PAIRS):
            side, chip = place(meta, s, p)
            for slot in range(2):
                low, high = tile_of(prod.at[2 * slot], k, l, False), tile_of(prod.at[2 * slot + 1], k, l, True)
                acc[side, chip, pl.ds(64 * slot, 64)] += jnp.where(lane, low, high)
            acc[side, chip, pl.ds(128, 32)] += folded(prod.at[4], k, l, lane[:32])
    outs += [pltpu.make_async_copy(acc.at[1], send, osem.at[2]), pltpu.make_async_copy(acc.at[0], keep, osem.at[3])]
    for c in outs[2:]:
        c.start()
    for c in outs:
        c.wait()


def far_kernel(pos, member, target, *refs):
    *refs, meta = refs
    prepare(pos, member, target, meta)
    up, down = refs[:CHUNKS], refs[CHUNKS : 2 * CHUNKS]
    f_in, n_in = refs[2 * CHUNKS : 2 + 2 * CHUNKS]
    keep, send = refs[2 + 2 * CHUNKS : 4 + 2 * CHUNKS]
    x, f3, near, left, right, prod, acc, isem, xsem, osem = refs[4 + 2 * CHUNKS :]
    copies = []
    ins = (
        (f_in, f3.at[:, pl.ds(0, 1024)]),
        (f_in.at[:, pl.ds(0, 512)], f3.at[:, pl.ds(1024, 512)]),
        (n_in, near.at[:, :, :, pl.ds(512, 1024)]),
        (n_in.at[:, :, :, pl.ds(0, 512)], near.at[:, :, :, pl.ds(0, 512)]),
    )
    xcopies = []
    for i, (a, b) in enumerate(ins):
        copies.append(pltpu.make_async_copy(a, b, isem.at[i]))
    for c in copies[:2]:
        c.start()
    for piece in range(2):
        for b in range(8):
            src = (up, down)[piece][SPOTS[b][0]].at[SPOTS[b][1]]
            c = pltpu.make_async_copy(src, x.at[piece, meta[2 + b]], xsem.at[piece * 8 + b])
            c.start()
            xcopies.append(c)
    for c in copies[2:]:
        c.start()
    acc[...] = jnp.zeros_like(acc)
    for c in copies[:2]:
        c.wait()
    for piece in range(2):
        for b in range(8):
            xcopies[piece * 8 + b].wait()
        for s in range(2):
            high, low = scale(x.at[piece], f3, s)
            if piece == 0:
                put(left, (s,), (high, high, low))
            put(right, (piece, s), (high, low, high))
    for c in copies[2:]:
        c.wait()
    lane = low_lanes((64, 128))
    for s in range(2):
        prod[0] = pairwise(left[s], right[1, s])
        prod[1] = pairwise(near[1, s], right[0, s])
        prod[2] = pairwise(near[0, s], right[1, s])
        for p, (k, l) in enumerate(PAIRS):
            side, chip = place(meta, s, p)
            acc[side, chip, pl.ds(64, 32)] += folded(prod.at[0], k, l, lane[:32])
            acc[side, chip, pl.ds(0, 64)] += jnp.where(lane, tile_of(prod.at[1], k, l, False), tile_of(prod.at[2], k, l, True))
    out = [pltpu.make_async_copy(acc.at[1], send, osem.at[0]), pltpu.make_async_copy(acc.at[0], keep, osem.at[1])]
    for c in out:
        c.start()
    for c in out:
        c.wait()


def final_kernel(meta, anc, near, eu, ed, far, du, dd, cd, out, acc):
    z = meta[0]
    acc[...] = jnp.zeros_like(acc)
    lane = lax.broadcasted_iota(jnp.int32, (64, 128), 1) // 64

    def add(src, half, d, rows):
        m = (z + d) & 7
        v = jnp.where((m & 1) == half, src, pltpu.roll(src, 64, 1))
        acc[m >> 1, rows] += jnp.where(lane[: v.shape[0]] == (m & 1), v, 0.0)

    every, top, bottom = pl.ds(0, 64), pl.ds(0, 32), pl.ds(32, 32)
    e1 = near[pl.ds(0, 64)]
    for src, half, d in ((e1, 0, -1), (e1, 1, 1), (eu[...], 0, -2), (ed[...], 1, 2), (du[...], 0, -3), (dd[...], 1, 3)):
        add(src, half, d, every)
    for src, d in ((near[pl.ds(128, 32)], 0), (cd[...], 4)):
        add(src, 0, d, top)
        add(src, 1, d, bottom)
    for q in range(4):
        cols = pl.ds(q * 128, 128)
        out[0, :, cols] = anc[0, :, cols] - acc[q]


def level(panels, factors, member, target, ancestors):
    wide = lax.axis_index("wide")
    z = lax.axis_index("narrow")
    scalars = (jnp.stack([z, wide]).astype(jnp.int32), member.T, target.T)

    def along(x, d):
        return lax.ppermute(x, "narrow", [(i, (i + d) % 8) for i in range(8)])

    def swap(x):
        return lax.ppermute(x, "wide", [(i, i ^ 1) for i in range(32)])

    def scatter(x):
        groups = [[2 * i + c for i in range(16)] for c in range(2)]
        return lax.all_to_all(x, "wide", 0, 0, axis_index_groups=groups, tiled=True)

    chunks = [panels[BOUNDS[c] : BOUNDS[c + 1]] for c in range(CHUNKS)]
    fu, fd = [factors], [factors]
    for _ in range(3):
        fu.append(along(fu[-1], 1))
        fd.append(along(fd[-1], -1))
    fu4 = along(fu[3][:1], 1)
    fd4 = along(fd[3][1:], -1)
    u1 = [along(c, 1) for c in chunks]
    d1 = [along(c, -1) for c in chunks]
    u2 = [along(c, 1) for c in u1]
    d2 = [along(c, -1) for c in d1]

    early = jax.ShapeDtypeStruct((16, 160, 128), F32)
    late = jax.ShapeDtypeStruct((16, 96, 128), F32)
    factor = jax.ShapeDtypeStruct((2, 1024, 512), BF)
    rows = jax.ShapeDtypeStruct((2, 2, 256, 1024), BF)
    dma = pltpu.SemaphoreType.DMA
    near = pl.pallas_call(
        near_kernel,
        name="near",
        out_shape=(early, early, factor, rows),
        in_specs=[SMEM] * 3 + [ANY] * (10 + 2 * CHUNKS),
        out_specs=(ANY,) * 4,
        scratch_shapes=[
            pltpu.VMEM((3, 8, 64, 512), F32),
            pltpu.VMEM((2, 512, 512), F32),
            pltpu.VMEM((2, 1536, 512), BF),
            pltpu.VMEM((3, 2, 256, 1536), BF),
            pltpu.VMEM((3, 2, 256, 1536), BF),
            pltpu.VMEM((5, 256, 256), F32),
            pltpu.VMEM((2, 16, 160, 128), F32),
            dma((9,)),
            dma((24,)),
            dma((4,)),
            pltpu.SMEM((30,), jnp.int32),
        ],
    )
    keep1, send1, f3, n3 = near(*scalars, panels, *u1, *d1, factors, fu[1], fd[1], fu[2], fd[2], fu[3], fd[3], fd4, fu4)
    r1 = jnp.sum(scatter(keep1 + swap(send1)), axis=0)
    eu, ed = along(r1[64:128], 1), along(r1[64:128], -1)

    far = pl.pallas_call(
        far_kernel,
        name="far",
        compiler_params=pltpu.CompilerParams(vmem_limit_bytes=24 << 20),
        out_shape=(late, late),
        in_specs=[SMEM] * 3 + [ANY] * (2 + 2 * CHUNKS),
        out_specs=(ANY,) * 2,
        scratch_shapes=[
            pltpu.VMEM((2, 8, 64, 512), F32),
            pltpu.VMEM((2, 1536, 512), BF),
            pltpu.VMEM((2, 2, 256, 1536), BF),
            pltpu.VMEM((2, 256, 1536), BF),
            pltpu.VMEM((2, 2, 256, 1536), BF),
            pltpu.VMEM((3, 256, 256), F32),
            pltpu.VMEM((2, 16, 96, 128), F32),
            dma((4,)),
            dma((16,)),
            dma((2,)),
            pltpu.SMEM((30,), jnp.int32),
        ],
    )
    keep2, send2 = far(*scalars, *u2, *d2, f3, n3)
    r2 = jnp.sum(scatter(keep2 + swap(send2)), axis=0)
    side, own = r2[:64], r2[64:]
    du, dd, cd = along(side, 1), along(side, -1), along(own, -2)
    return pl.pallas_call(
        final_kernel,
        name="final",
        out_shape=jax.ShapeDtypeStruct((1, 64, 512), F32),
        in_specs=[SMEM] + [VMEM] * 8,
        out_specs=VMEM,
        scratch_shapes=[pltpu.VMEM((4, 64, 128), F32)],
    )(scalars[0], ancestors, r1, eu, ed, r2, du, dd, cd)


def solution(mesh):
    return jax.shard_map(
        level,
        mesh=mesh,
        in_specs=(
            P("wide", "narrow", None),
            P("wide", "narrow", None),
            P(),
            P(),
            P("wide", "narrow", None),
        ),
        out_specs=P("wide", "narrow", None),
        check_vma=False,
    )
```

```python
import jax
import jax.numpy as jnp
from jax import lax
from jax.experimental import pallas as pl
from jax.experimental.pallas import tpu as pltpu
from jax.sharding import PartitionSpec as P


PAIRS = tuple((k, l) for k in range(4) for l in range(k + 1))
BOUNDS = (0, 2, 4, 8)
FAR_BOUNDS = (0, 4, 8)
CHUNKS, FAR_CHUNKS = len(BOUNDS) - 1, len(FAR_BOUNDS) - 1


def spots(bounds):
    return tuple((c, b - bounds[c]) for c in range(len(bounds) - 1) for b in range(bounds[c], bounds[c + 1]))


SPOTS, FAR_SPOTS = spots(BOUNDS), spots(FAR_BOUNDS)
ANY = pl.BlockSpec(memory_space=pltpu.HBM)
SMEM = pl.BlockSpec(memory_space=pltpu.SMEM)
VMEM = pl.BlockSpec(memory_space=pltpu.VMEM)
BF, F32 = jnp.bfloat16, jnp.float32


def split(x):
    high = x.astype(BF)
    return high, (x - high.astype(F32)).astype(BF)


def low_lanes(shape):
    return lax.broadcasted_iota(jnp.int32, shape, 1) < 64


def prepare(pos, member, target, meta):
    wide = pos[1]
    meta[0] = pos[0]
    meta[1] = wide & 1
    for s in range(2):
        for k in range(4):
            meta[2 + member[k, 2 * wide + s] - 8 * wide] = 4 * s + k
        for p in range(10):
            meta[10 + 10 * s + p] = target[p, 2 * wide + s]


def place(meta, s, p):
    tile = meta[10 + s * 10 + p]
    return (tile + meta[1]) & 1, tile >> 1


def scale(x_ref, f3, s):
    xh, xl = split(x_ref[pl.ds(4 * s, 4)].reshape(256, 512))
    x3 = jnp.concatenate([xh, xh, xl], axis=1)
    return split(lax.dot_general(x3, f3[s], (((1,), (0,)), ((), ())), preferred_element_type=F32))


def put(ref, index, parts):
    for i, part in enumerate(parts):
        ref[(*index, slice(None), pl.ds(512 * i, 512))] = part


def pairwise(left, right):
    return lax.dot_general(left, right, (((1,), (1,)), ((), ())), preferred_element_type=F32)


def tile_of(prod, k, l, upper):
    v = prod[pl.ds(k * 64, 64), pl.ds((l // 2) * 128, 128)]
    return v if (l % 2 == 1) == upper else pltpu.roll(v, 64, 1)


def folded(prod, k, l, lane):
    low, high = tile_of(prod, k, l, False), tile_of(prod, k, l, True)
    return jnp.where(lane, low[:32], high[32:])


def near_kernel(pos, member, target, *refs):
    *refs, meta = refs
    prepare(pos, member, target, meta)
    panels, up, down = refs[0], refs[1 : 1 + CHUNKS], refs[1 + CHUNKS : 1 + 2 * CHUNKS]
    fac = refs[1 + 2 * CHUNKS : 9 + 2 * CHUNKS]
    fu4 = refs[9 + 2 * CHUNKS]
    keep, send, f_out, n_out = refs[10 + 2 * CHUNKS : 14 + 2 * CHUNKS]
    x, f, f3, left, right, prod, acc, fsem, xsem, osem = refs[14 + 2 * CHUNKS :]
    z = meta[0]
    fcopies = []
    for i, (ref, d) in enumerate(zip(fac[:7], (0, -1, 1, -2, 2, -3, 3))):
        rows = pl.ds(pl.multiple_of(((z + d) & 7) * 64, 64), 64)
        fcopies.append(pltpu.make_async_copy(ref, f.at[:, rows], fsem.at[i]))
    rows4 = pl.ds(pl.multiple_of(((z + 4) & 7) * 64, 64), 64)
    fcopies.append(pltpu.make_async_copy(fu4, f.at[pl.ds(0, 1), rows4], fsem.at[7]))
    fcopies.append(pltpu.make_async_copy(fac[7], f.at[pl.ds(1, 1), rows4], fsem.at[8]))
    for c in fcopies:
        c.start()
    xcopies = []
    for piece in range(3):
        for b in range(8):
            src = panels.at[b] if piece == 0 else (up, down)[piece - 1][SPOTS[b][0]].at[SPOTS[b][1]]
            c = pltpu.make_async_copy(src, x.at[piece, meta[2 + b]], xsem.at[piece * 8 + b])
            c.start()
            xcopies.append(c)
    acc[...] = jnp.zeros_like(acc)
    for c in fcopies:
        c.wait()
    for s in range(2):
        high, low = split(f[s])
        for i, part in enumerate((high, low, high)):
            f3[s, pl.ds(512 * i, 512)] = part
    outs = [pltpu.make_async_copy(f3.at[:, pl.ds(0, 1024)], f_out, osem.at[0])]
    outs[0].start()
    for piece in range(3):
        for b in range(8):
            xcopies[piece * 8 + b].wait()
        for s in range(2):
            high, low = scale(x.at[piece], f3, s)
            put(left, (piece, s), (high, high, low))
            put(right, (piece, s), (high, low, high))
    outs.append(pltpu.make_async_copy(left.at[pl.ds(1, 2), :, :, pl.ds(512, 1024)], n_out, osem.at[1]))
    outs[1].start()
    lane = low_lanes((64, 128))
    for s in range(2):
        prod[0] = pairwise(left[0, s], right[1, s])
        prod[1] = pairwise(left[0, s], right[2, s])
        prod[2] = pairwise(left[2, s], right[1, s])
        prod[3] = pairwise(left[1, s], right[2, s])
        prod[4] = pairwise(left[0, s], right[0, s])
        for p, (k, l) in enumerate(PAIRS):
            side, chip = place(meta, s, p)
            for slot in range(2):
                low, high = tile_of(prod.at[2 * slot], k, l, False), tile_of(prod.at[2 * slot + 1], k, l, True)
                acc[side, chip, pl.ds(64 * slot, 64)] += jnp.where(lane, low, high)
            acc[side, chip, pl.ds(128, 32)] += folded(prod.at[4], k, l, lane[:32])
    outs += [pltpu.make_async_copy(acc.at[1], send, osem.at[2]), pltpu.make_async_copy(acc.at[0], keep, osem.at[3])]
    for c in outs[2:]:
        c.start()
    for c in outs:
        c.wait()


def far_kernel(pos, member, target, *refs):
    *refs, meta = refs
    prepare(pos, member, target, meta)
    up, down = refs[:FAR_CHUNKS], refs[FAR_CHUNKS : 2 * FAR_CHUNKS]
    f_in, n_in = refs[2 * FAR_CHUNKS : 2 + 2 * FAR_CHUNKS]
    keep, send = refs[2 + 2 * FAR_CHUNKS : 4 + 2 * FAR_CHUNKS]
    x, f3, near, left, right, prod, acc, isem, xsem, osem = refs[4 + 2 * FAR_CHUNKS :]
    copies = []
    ins = (
        (f_in, f3.at[:, pl.ds(0, 1024)]),
        (f_in.at[:, pl.ds(0, 512)], f3.at[:, pl.ds(1024, 512)]),
        (n_in, near.at[:, :, :, pl.ds(512, 1024)]),
        (n_in.at[:, :, :, pl.ds(0, 512)], near.at[:, :, :, pl.ds(0, 512)]),
    )
    xcopies = []
    for i, (a, b) in enumerate(ins):
        copies.append(pltpu.make_async_copy(a, b, isem.at[i]))
    for c in copies[:2]:
        c.start()
    for piece in range(2):
        for b in range(8):
            src = (up, down)[piece][FAR_SPOTS[b][0]].at[FAR_SPOTS[b][1]]
            c = pltpu.make_async_copy(src, x.at[piece, meta[2 + b]], xsem.at[piece * 8 + b])
            c.start()
            xcopies.append(c)
    for c in copies[2:]:
        c.start()
    acc[...] = jnp.zeros_like(acc)
    for c in copies[:2]:
        c.wait()
    for piece in range(2):
        for b in range(8):
            xcopies[piece * 8 + b].wait()
        for s in range(2):
            high, low = scale(x.at[piece], f3, s)
            if piece == 0:
                put(left, (s,), (high, high, low))
            put(right, (piece, s), (high, low, high))
    for c in copies[2:]:
        c.wait()
    lane = low_lanes((64, 128))
    for s in range(2):
        prod[0] = pairwise(left[s], right[1, s])
        prod[1] = pairwise(near[1, s], right[0, s])
        prod[2] = pairwise(near[0, s], right[1, s])
        for p, (k, l) in enumerate(PAIRS):
            side, chip = place(meta, s, p)
            acc[side, chip, pl.ds(64, 32)] += folded(prod.at[0], k, l, lane[:32])
            acc[side, chip, pl.ds(0, 64)] += jnp.where(lane, tile_of(prod.at[1], k, l, False), tile_of(prod.at[2], k, l, True))
    out = [pltpu.make_async_copy(acc.at[1], send, osem.at[0]), pltpu.make_async_copy(acc.at[0], keep, osem.at[1])]
    for c in out:
        c.start()
    for c in out:
        c.wait()


def final_kernel(meta, anc, near, eu, ed, far, du, dd, cd, out, acc):
    z = meta[0]
    acc[...] = jnp.zeros_like(acc)
    lane = lax.broadcasted_iota(jnp.int32, (64, 128), 1) // 64

    def add(src, half, d, rows):
        m = (z + d) & 7
        v = jnp.where((m & 1) == half, src, pltpu.roll(src, 64, 1))
        acc[m >> 1, rows] += jnp.where(lane[: v.shape[0]] == (m & 1), v, 0.0)

    every, top, bottom = pl.ds(0, 64), pl.ds(0, 32), pl.ds(32, 32)
    e1 = near[pl.ds(0, 64)]
    for src, half, d in ((e1, 0, -1), (e1, 1, 1), (eu[...], 0, -2), (ed[...], 1, 2), (du[...], 0, -3), (dd[...], 1, 3)):
        add(src, half, d, every)
    for src, d in ((near[pl.ds(128, 32)], 0), (cd[...], 4)):
        add(src, 0, d, top)
        add(src, 1, d, bottom)
    for q in range(4):
        cols = pl.ds(q * 128, 128)
        out[0, :, cols] = anc[0, :, cols] - acc[q]


def level(panels, factors, member, target, ancestors):
    wide = lax.axis_index("wide")
    z = lax.axis_index("narrow")
    scalars = (jnp.stack([z, wide]).astype(jnp.int32), member.T, target.T)

    def along(x, d):
        return lax.ppermute(x, "narrow", [(i, (i + d) % 8) for i in range(8)])

    def swap(x):
        return lax.ppermute(x, "wide", [(i, i ^ 1) for i in range(32)])

    def scatter(x):
        groups = [[2 * i + c for i in range(16)] for c in range(2)]
        return lax.all_to_all(x, "wide", 0, 0, axis_index_groups=groups, tiled=True)

    chunks = [panels[BOUNDS[c] : BOUNDS[c + 1]] for c in range(CHUNKS)]
    fu, fd = [factors], [factors]
    for _ in range(3):
        fu.append(along(fu[-1], 1))
        fd.append(along(fd[-1], -1))
    fu4 = along(fu[3][:1], 1)
    fd4 = along(fd[3][1:], -1)
    u1 = [along(c, 1) for c in chunks]
    d1 = [along(c, -1) for c in chunks]

    def joined(pieces, c):
        parts = [p for p, low, high in zip(pieces, BOUNDS, BOUNDS[1:]) if FAR_BOUNDS[c] <= low and high <= FAR_BOUNDS[c + 1]]
        return parts[0] if len(parts) == 1 else jnp.concatenate(parts)

    u2 = [along(joined(u1, c), 1) for c in range(FAR_CHUNKS)]
    d2 = [along(joined(d1, c), -1) for c in range(FAR_CHUNKS)]

    early = jax.ShapeDtypeStruct((16, 160, 128), F32)
    late = jax.ShapeDtypeStruct((16, 96, 128), F32)
    factor = jax.ShapeDtypeStruct((2, 1024, 512), BF)
    rows = jax.ShapeDtypeStruct((2, 2, 256, 1024), BF)
    dma = pltpu.SemaphoreType.DMA
    near = pl.pallas_call(
        near_kernel,
        name="near",
        out_shape=(early, early, factor, rows),
        in_specs=[SMEM] * 3 + [ANY] * (10 + 2 * CHUNKS),
        out_specs=(ANY,) * 4,
        scratch_shapes=[
            pltpu.VMEM((3, 8, 64, 512), F32),
            pltpu.VMEM((2, 512, 512), F32),
            pltpu.VMEM((2, 1536, 512), BF),
            pltpu.VMEM((3, 2, 256, 1536), BF),
            pltpu.VMEM((3, 2, 256, 1536), BF),
            pltpu.VMEM((5, 256, 256), F32),
            pltpu.VMEM((2, 16, 160, 128), F32),
            dma((9,)),
            dma((24,)),
            dma((4,)),
            pltpu.SMEM((30,), jnp.int32),
        ],
    )
    keep1, send1, f3, n3 = near(*scalars, panels, *u1, *d1, factors, fu[1], fd[1], fu[2], fd[2], fu[3], fd[3], fd4, fu4)
    r1 = jnp.sum(scatter(keep1 + swap(send1)), axis=0)
    eu, ed = along(r1[64:128], 1), along(r1[64:128], -1)

    far = pl.pallas_call(
        far_kernel,
        name="far",
        compiler_params=pltpu.CompilerParams(vmem_limit_bytes=24 << 20),
        out_shape=(late, late),
        in_specs=[SMEM] * 3 + [ANY] * (2 + 2 * FAR_CHUNKS),
        out_specs=(ANY,) * 2,
        scratch_shapes=[
            pltpu.VMEM((2, 8, 64, 512), F32),
            pltpu.VMEM((2, 1536, 512), BF),
            pltpu.VMEM((2, 2, 256, 1536), BF),
            pltpu.VMEM((2, 256, 1536), BF),
            pltpu.VMEM((2, 2, 256, 1536), BF),
            pltpu.VMEM((3, 256, 256), F32),
            pltpu.VMEM((2, 16, 96, 128), F32),
            dma((4,)),
            dma((16,)),
            dma((2,)),
            pltpu.SMEM((30,), jnp.int32),
        ],
    )
    keep2, send2 = far(*scalars, *u2, *d2, f3, n3)
    r2 = jnp.sum(scatter(keep2 + swap(send2)), axis=0)
    side, own = r2[:64], r2[64:]
    du, dd, cd = along(side, 1), along(side, -1), along(own, -2)
    return pl.pallas_call(
        final_kernel,
        name="final",
        compiler_params=pltpu.CompilerParams(vmem_limit_bytes=4 << 20),
        out_shape=jax.ShapeDtypeStruct((1, 64, 512), F32),
        in_specs=[SMEM] + [VMEM] * 8,
        out_specs=VMEM,
        scratch_shapes=[pltpu.VMEM((4, 64, 128), F32)],
    )(scalars[0], ancestors, r1, eu, ed, r2, du, dd, cd)


def solution(mesh):
    return jax.shard_map(
        level,
        mesh=mesh,
        in_specs=(
            P("wide", "narrow", None),
            P("wide", "narrow", None),
            P(),
            P(),
            P("wide", "narrow", None),
        ),
        out_specs=P("wide", "narrow", None),
        check_vma=False,
    )
```

```python
import jax
import jax.numpy as jnp
from jax import lax
from jax.experimental import pallas as pl
from jax.experimental.pallas import tpu as pltpu
from jax.sharding import PartitionSpec as P


PAIRS = tuple((k, l) for k in range(4) for l in range(k + 1))
BOUNDS = (0, 2, 4, 8)
FAR_BOUNDS = (0, 4, 8)
CHUNKS, FAR_CHUNKS = len(BOUNDS) - 1, len(FAR_BOUNDS) - 1


def spots(bounds):
    return tuple((c, b - bounds[c]) for c in range(len(bounds) - 1) for b in range(bounds[c], bounds[c + 1]))


SPOTS, FAR_SPOTS = spots(BOUNDS), spots(FAR_BOUNDS)
ANY = pl.BlockSpec(memory_space=pltpu.HBM)
SMEM = pl.BlockSpec(memory_space=pltpu.SMEM)
VMEM = pl.BlockSpec(memory_space=pltpu.VMEM)
BF, F32 = jnp.bfloat16, jnp.float32


def split(x):
    high = x.astype(BF)
    return high, (x - high.astype(F32)).astype(BF)


def low_lanes(shape):
    return lax.broadcasted_iota(jnp.int32, shape, 1) < 64


def prepare(pos, member, target, meta):
    wide = pos[1]
    meta[0] = pos[0]
    meta[1] = wide & 1
    for s in range(2):
        for k in range(4):
            meta[2 + member[k, 2 * wide + s] - 8 * wide] = 4 * s + k
        for p in range(10):
            meta[10 + 10 * s + p] = target[p, 2 * wide + s]


def place(meta, s, p):
    tile = meta[10 + s * 10 + p]
    first, second = tile >> 3, (tile >> 1) & 3
    return (tile + meta[1]) & 1, jnp.where((tile & 1) == 0, ((first - second) & 3) * 4 + second, ((second - first) & 3) * 4 + first)


def scale(x_ref, f3, s):
    xh, xl = split(x_ref[pl.ds(4 * s, 4)].reshape(256, 512))
    x3 = jnp.concatenate([xh, xh, xl], axis=1)
    return split(lax.dot_general(x3, f3[s], (((1,), (0,)), ((), ())), preferred_element_type=F32))


def put(ref, index, parts):
    for i, part in enumerate(parts):
        ref[(*index, slice(None), pl.ds(512 * i, 512))] = part


def pairwise(left, right):
    return lax.dot_general(left, right, (((1,), (1,)), ((), ())), preferred_element_type=F32)


def tile_of(prod, k, l, upper):
    v = prod[pl.ds(k * 64, 64), pl.ds((l // 2) * 128, 128)]
    return v if (l % 2 == 1) == upper else pltpu.roll(v, 64, 1)


def folded(prod, k, l, lane):
    low, high = tile_of(prod, k, l, False), tile_of(prod, k, l, True)
    return jnp.where(lane, low[:32], high[32:])


def near_kernel(pos, member, target, *refs):
    *refs, meta = refs
    prepare(pos, member, target, meta)
    panels, up, down = refs[0], refs[1 : 1 + CHUNKS], refs[1 + CHUNKS : 1 + 2 * CHUNKS]
    fac = refs[1 + 2 * CHUNKS : 9 + 2 * CHUNKS]
    fu4 = refs[9 + 2 * CHUNKS]
    keep, send, f_out, n_out = refs[10 + 2 * CHUNKS : 14 + 2 * CHUNKS]
    x, f, f3, left, right, prod, acc, fsem, xsem, osem = refs[14 + 2 * CHUNKS :]
    z = meta[0]
    fcopies = []
    for i, (ref, d) in enumerate(zip(fac[:7], (0, -1, 1, -2, 2, -3, 3))):
        rows = pl.ds(pl.multiple_of(((z + d) & 7) * 64, 64), 64)
        fcopies.append(pltpu.make_async_copy(ref, f.at[:, rows], fsem.at[i]))
    rows4 = pl.ds(pl.multiple_of(((z + 4) & 7) * 64, 64), 64)
    fcopies.append(pltpu.make_async_copy(fu4, f.at[pl.ds(0, 1), rows4], fsem.at[7]))
    fcopies.append(pltpu.make_async_copy(fac[7], f.at[pl.ds(1, 1), rows4], fsem.at[8]))
    for c in fcopies:
        c.start()
    xcopies = []
    for piece in range(3):
        for b in range(8):
            src = panels.at[b] if piece == 0 else (up, down)[piece - 1][SPOTS[b][0]].at[SPOTS[b][1]]
            c = pltpu.make_async_copy(src, x.at[piece, meta[2 + b]], xsem.at[piece * 8 + b])
            c.start()
            xcopies.append(c)
    acc[...] = jnp.zeros_like(acc)
    for c in fcopies:
        c.wait()
    for s in range(2):
        high, low = split(f[s])
        for i, part in enumerate((high, low, high)):
            f3[s, pl.ds(512 * i, 512)] = part
    outs = [pltpu.make_async_copy(f3.at[:, pl.ds(0, 1024)], f_out, osem.at[0])]
    outs[0].start()
    for piece in range(3):
        for b in range(8):
            xcopies[piece * 8 + b].wait()
        for s in range(2):
            high, low = scale(x.at[piece], f3, s)
            put(left, (piece, s), (high, high, low))
            put(right, (piece, s), (high, low, high))
    outs.append(pltpu.make_async_copy(left.at[pl.ds(1, 2), :, :, pl.ds(512, 1024)], n_out, osem.at[1]))
    outs[1].start()
    lane = low_lanes((64, 128))
    for s in range(2):
        prod[0] = pairwise(left[0, s], right[1, s])
        prod[1] = pairwise(left[0, s], right[2, s])
        prod[2] = pairwise(left[2, s], right[1, s])
        prod[3] = pairwise(left[1, s], right[2, s])
        prod[4] = pairwise(left[0, s], right[0, s])
        for p, (k, l) in enumerate(PAIRS):
            side, chip = place(meta, s, p)
            for slot in range(2):
                low, high = tile_of(prod.at[2 * slot], k, l, False), tile_of(prod.at[2 * slot + 1], k, l, True)
                acc[side, chip, pl.ds(64 * slot, 64)] += jnp.where(lane, low, high)
            acc[side, chip, pl.ds(128, 32)] += folded(prod.at[4], k, l, lane[:32])
    outs += [pltpu.make_async_copy(acc.at[1], send, osem.at[2]), pltpu.make_async_copy(acc.at[0], keep, osem.at[3])]
    for c in outs[2:]:
        c.start()
    for c in outs:
        c.wait()


def far_kernel(pos, member, target, *refs):
    *refs, meta = refs
    prepare(pos, member, target, meta)
    up, down = refs[:FAR_CHUNKS], refs[FAR_CHUNKS : 2 * FAR_CHUNKS]
    f_in, n_in = refs[2 * FAR_CHUNKS : 2 + 2 * FAR_CHUNKS]
    keep, send = refs[2 + 2 * FAR_CHUNKS : 4 + 2 * FAR_CHUNKS]
    x, f3, near, left, right, prod, acc, isem, xsem, osem = refs[4 + 2 * FAR_CHUNKS :]
    copies = []
    ins = (
        (f_in, f3.at[:, pl.ds(0, 1024)]),
        (f_in.at[:, pl.ds(0, 512)], f3.at[:, pl.ds(1024, 512)]),
        (n_in, near.at[:, :, :, pl.ds(512, 1024)]),
        (n_in.at[:, :, :, pl.ds(0, 512)], near.at[:, :, :, pl.ds(0, 512)]),
    )
    xcopies = []
    for i, (a, b) in enumerate(ins):
        copies.append(pltpu.make_async_copy(a, b, isem.at[i]))
    for c in copies[:2]:
        c.start()
    for piece in range(2):
        for b in range(8):
            src = (up, down)[piece][FAR_SPOTS[b][0]].at[FAR_SPOTS[b][1]]
            c = pltpu.make_async_copy(src, x.at[piece, meta[2 + b]], xsem.at[piece * 8 + b])
            c.start()
            xcopies.append(c)
    for c in copies[2:]:
        c.start()
    acc[...] = jnp.zeros_like(acc)
    for c in copies[:2]:
        c.wait()
    for piece in range(2):
        for b in range(8):
            xcopies[piece * 8 + b].wait()
        for s in range(2):
            high, low = scale(x.at[piece], f3, s)
            if piece == 0:
                put(left, (s,), (high, high, low))
            put(right, (piece, s), (high, low, high))
    for c in copies[2:]:
        c.wait()
    lane = low_lanes((64, 128))
    for s in range(2):
        prod[0] = pairwise(left[s], right[1, s])
        prod[1] = pairwise(near[1, s], right[0, s])
        prod[2] = pairwise(near[0, s], right[1, s])
        for p, (k, l) in enumerate(PAIRS):
            side, chip = place(meta, s, p)
            acc[side, chip, pl.ds(64, 32)] += folded(prod.at[0], k, l, lane[:32])
            acc[side, chip, pl.ds(0, 64)] += jnp.where(lane, tile_of(prod.at[1], k, l, False), tile_of(prod.at[2], k, l, True))
    out = [pltpu.make_async_copy(acc.at[1], send, osem.at[0]), pltpu.make_async_copy(acc.at[0], keep, osem.at[1])]
    for c in out:
        c.start()
    for c in out:
        c.wait()


def final_kernel(meta, anc, near, eu, ed, far, du, dd, cd, out, acc):
    z = meta[0]
    acc[...] = jnp.zeros_like(acc)
    lane = lax.broadcasted_iota(jnp.int32, (64, 128), 1) // 64

    def add(src, half, d, rows):
        m = (z + d) & 7
        v = jnp.where((m & 1) == half, src, pltpu.roll(src, 64, 1))
        acc[m >> 1, rows] += jnp.where(lane[: v.shape[0]] == (m & 1), v, 0.0)

    every, top, bottom = pl.ds(0, 64), pl.ds(0, 32), pl.ds(32, 32)
    e1 = near[pl.ds(0, 64)]
    for src, half, d in ((e1, 0, -1), (e1, 1, 1), (eu[...], 0, -2), (ed[...], 1, 2), (du[...], 0, -3), (dd[...], 1, 3)):
        add(src, half, d, every)
    for src, d in ((near[pl.ds(128, 32)], 0), (cd[...], 4)):
        add(src, 0, d, top)
        add(src, 1, d, bottom)
    for q in range(4):
        cols = pl.ds(q * 128, 128)
        out[0, :, cols] = anc[0, :, cols] - acc[q]


def level(panels, factors, member, target, ancestors):
    wide = lax.axis_index("wide")
    z = lax.axis_index("narrow")
    scalars = (jnp.stack([z, wide]).astype(jnp.int32), member.T, target.T)

    def along(x, d):
        return lax.ppermute(x, "narrow", [(i, (i + d) % 8) for i in range(8)])

    def swap(x):
        return lax.ppermute(x, "wide", [(i, i ^ 1) for i in range(32)])

    def scatter(x):
        groups = [
            [((a + y) % 4 * 4 + y) * 2 for a in range(4) for y in range(4)],
            [(x * 4 + (a + x) % 4) * 2 + 1 for a in range(4) for x in range(4)],
        ]
        return lax.all_to_all(x, "wide", 0, 0, axis_index_groups=groups, tiled=True)

    chunks = [panels[BOUNDS[c] : BOUNDS[c + 1]] for c in range(CHUNKS)]
    fu, fd = [factors], [factors]
    for _ in range(3):
        fu.append(along(fu[-1], 1))
        fd.append(along(fd[-1], -1))
    fu4 = along(fu[3][:1], 1)
    fd4 = along(fd[3][1:], -1)
    u1 = [along(c, 1) for c in chunks]
    d1 = [along(c, -1) for c in chunks]

    def joined(pieces, c):
        parts = [p for p, low, high in zip(pieces, BOUNDS, BOUNDS[1:]) if FAR_BOUNDS[c] <= low and high <= FAR_BOUNDS[c + 1]]
        return parts[0] if len(parts) == 1 else jnp.concatenate(parts)

    u2 = [along(joined(u1, c), 1) for c in range(FAR_CHUNKS)]
    d2 = [along(joined(d1, c), -1) for c in range(FAR_CHUNKS)]

    early = jax.ShapeDtypeStruct((16, 160, 128), F32)
    late = jax.ShapeDtypeStruct((16, 96, 128), F32)
    factor = jax.ShapeDtypeStruct((2, 1024, 512), BF)
    rows = jax.ShapeDtypeStruct((2, 2, 256, 1024), BF)
    dma = pltpu.SemaphoreType.DMA
    near = pl.pallas_call(
        near_kernel,
        name="near",
        out_shape=(early, early, factor, rows),
        in_specs=[SMEM] * 3 + [ANY] * (10 + 2 * CHUNKS),
        out_specs=(ANY,) * 4,
        scratch_shapes=[
            pltpu.VMEM((3, 8, 64, 512), F32),
            pltpu.VMEM((2, 512, 512), F32),
            pltpu.VMEM((2, 1536, 512), BF),
            pltpu.VMEM((3, 2, 256, 1536), BF),
            pltpu.VMEM((3, 2, 256, 1536), BF),
            pltpu.VMEM((5, 256, 256), F32),
            pltpu.VMEM((2, 16, 160, 128), F32),
            dma((9,)),
            dma((24,)),
            dma((4,)),
            pltpu.SMEM((30,), jnp.int32),
        ],
    )
    keep1, send1, f3, n3 = near(*scalars, panels, *u1, *d1, factors, fu[1], fd[1], fu[2], fd[2], fu[3], fd[3], fd4, fu4)
    r1 = jnp.sum(scatter(keep1 + swap(send1)), axis=0)
    eu, ed = along(r1[64:128], 1), along(r1[64:128], -1)

    far = pl.pallas_call(
        far_kernel,
        name="far",
        compiler_params=pltpu.CompilerParams(vmem_limit_bytes=24 << 20),
        out_shape=(late, late),
        in_specs=[SMEM] * 3 + [ANY] * (2 + 2 * FAR_CHUNKS),
        out_specs=(ANY,) * 2,
        scratch_shapes=[
            pltpu.VMEM((2, 8, 64, 512), F32),
            pltpu.VMEM((2, 1536, 512), BF),
            pltpu.VMEM((2, 2, 256, 1536), BF),
            pltpu.VMEM((2, 256, 1536), BF),
            pltpu.VMEM((2, 2, 256, 1536), BF),
            pltpu.VMEM((3, 256, 256), F32),
            pltpu.VMEM((2, 16, 96, 128), F32),
            dma((4,)),
            dma((16,)),
            dma((2,)),
            pltpu.SMEM((30,), jnp.int32),
        ],
    )
    keep2, send2 = far(*scalars, *u2, *d2, f3, n3)
    r2 = jnp.sum(scatter(keep2 + swap(send2)), axis=0)
    side, own = r2[:64], r2[64:]
    du, dd, cd = along(side, 1), along(side, -1), along(own, -2)
    return pl.pallas_call(
        final_kernel,
        name="final",
        compiler_params=pltpu.CompilerParams(vmem_limit_bytes=4 << 20),
        out_shape=jax.ShapeDtypeStruct((1, 64, 512), F32),
        in_specs=[SMEM] + [VMEM] * 8,
        out_specs=VMEM,
        scratch_shapes=[pltpu.VMEM((4, 64, 128), F32)],
    )(scalars[0], ancestors, r1, eu, ed, r2, du, dd, cd)


def solution(mesh):
    return jax.shard_map(
        level,
        mesh=mesh,
        in_specs=(
            P("wide", "narrow", None),
            P("wide", "narrow", None),
            P(),
            P(),
            P("wide", "narrow", None),
        ),
        out_specs=P("wide", "narrow", None),
        check_vma=False,
    )
```
